32 devices in a mesh: dp: 2 (over core), seqo: 4 (over y, x), seqi: 4 (over z).
Axes of the slice: x: 2, y: 2, z: 4, core: 2. Of those that a mesh axis runs over, the one named last changes fastest.
Arguments:
- loaded: bfloat16 [4096, 1024], P(('dp', 'seqo', 'seqi')), parts along dimension 0, may hold values from -6 to 6
- packing: int32 [8, 4, 4, 2], P(('dp', 'seqo')), parts along dimension 0, may hold values from 0 to 128, as said below
- pattern: int32 [32, 64, 64], P(('dp', 'seqo', 'seqi')), parts along dimension 0, may hold values from 0 to 1, as said below
- w_query: bfloat16 [1024, 1024], replicated, may hold values from -0.1875 to 0.1875
- w_key: bfloat16 [1024, 1024], replicated, may hold values from -0.1875 to 0.1875
- w_value: bfloat16 [1024, 1024], replicated, may hold values from -0.1875 to 0.1875
- norm_gain: float32 [1024], replicated, may hold values from 0.25 to 1.75
- w_out: bfloat16 [1024, 1024], replicated, may hold values from -0.1875 to 0.1875
Outputs:
- mixed: float32 [4096, 1024], P(('dp', 'seqo', 'seqi')), parts along dimension 0
The draws below stay inside these ranges and needn't reach their ends.
There are 2 independent parts, one for each index of `dp`. The reference program is written for one: setup_inputs(seed, part) draws one part's arguments, and reference() takes and returns one part's arrays. A program takes and returns all parts, laid end to end along the dimension named above; an argument that names none is the same for every part. Nothing has to cross between parts.
Inputs may be any that keep to these rules, and one draw needn't show every extreme that they name: `packing`: for each group and source s the counts over d sum to 128 and the offsets are their running sums in the order of d; for each destination d the counts over s sum to 128; a count is at most 64, and some count of every group equals 64. pattern[c, i, j] is 1 where j == i and 0 where j > i.
All inputs are finite; a program needn't handle non-finite values.
Results may differ from the reference program's by a relative error of at most 0.0053.
Values may be sent and summed in bfloat16 or wider, within the bound.
No kernel may reach another device: no remote copies, remote signals or barrier semaphores. Data moves between devices by JAX's collectives and lax.ppermute only.
A program may use at most 128 MiB of HBM per device.

```python
import jax
import jax.numpy as jnp
from jax import lax

D = 1024
H = 16
HD = 64
NB = 64
TOK_DEV = 128
SPANS = 16
SEQ = 2048
N_SEQO = 4
N_SEQI = 4


def draw_packing(key, part):
    average = TOK_DEV // N_SEQI
    halves = N_SEQI // 2

    def one_group(group_key):
        subkeys = jax.random.split(group_key, 4)
        source_perm = jax.random.permutation(subkeys[0], N_SEQI)
        target_perm = jax.random.permutation(subkeys[1], N_SEQI)
        spread = jax.random.randint(subkeys[2], (halves,), -average, average + 1)
        spread = spread.at[0].set(average)
        weights = jnp.concatenate([average + spread, average - spread])
        weights = jax.random.permutation(subkeys[3], weights)
        latin = (source_perm[:, None] + target_perm[None, :]) % N_SEQI
        counts = weights[latin]
        offsets = jnp.cumsum(counts, axis=1) - counts
        return jnp.stack([offsets, counts], axis=-1).astype(jnp.int32)
    return jax.vmap(one_group)(jax.random.split(key, N_SEQO)).astype(jnp.int32)


def draw_pattern(key, part):
    level_key, random_key = jax.random.split(jax.random.fold_in(key, 7))
    level = jax.random.randint(level_key, (SPANS, 1, 1), 1, 8)
    draws = jax.random.randint(random_key, (SPANS, NB, NB), 0, 8)
    row_ids = jnp.arange(NB)[:, None]
    col_ids = jnp.arange(NB)[None, :]
    below = ((draws < level) & (col_ids < row_ids)).astype(jnp.int32)
    return (below + (col_ids == row_ids).astype(jnp.int32)).astype(jnp.int32)


def block_scale(rng, dims, pieces, smallest, top_value):
    factor_of, own = 1.0, jax.random.fold_in(rng, 6)
    for dim, shards_of in pieces:
        heights = jnp.exp(jax.random.uniform(jax.random.fold_in(own, dim), (shards_of,), jnp.float32, smallest / len(pieces), top_value / len(pieces)))
        factor_of = factor_of * jnp.repeat(heights, dims[dim] // shards_of).reshape([-1 if axis == dim else 1 for axis in range(len(dims))])
    return factor_of


def centred(rng, extent, deviation, most, cuts=(), held_as=jnp.bfloat16):
    entries = jax.random.normal(rng, extent, jnp.float32) * deviation
    if len(cuts) > 0:
        entries = block_scale(rng, extent, cuts, -0.22, 0.18) * entries
    return jnp.clip(entries, min=-most, max=most).astype(held_as)


def setup_inputs(seed: int = 0, part: int = 0) -> dict:
    keys = jax.random.split(jax.random.key(seed), 9)
    part_keys = jax.random.split(jax.random.fold_in(keys[8], part), 9)
    return {
        "loaded": centred(part_keys[0], (SEQ, D), 1.0, 6.0, ((0, 16),)),
        "packing": draw_packing(jax.random.fold_in(jax.random.fold_in(keys[8], part), 71), part),
        "pattern": draw_pattern(jax.random.fold_in(jax.random.fold_in(keys[8], part), 71), part),
        "w_query": centred(keys[3], (D, D), D ** -0.5, 0.1875),
        "w_key": centred(keys[4], (D, D), D ** -0.5, 0.1875),
        "w_value": centred(keys[5], (D, D), D ** -0.5, 0.1875),
        "norm_gain": jnp.clip(1.0 + 0.15 * jax.random.normal(keys[6], (D,), jnp.float32), 0.25, 1.75),
        "w_out": centred(keys[7], (D, D), D ** -0.5, 0.1875),
    }


EPSILON = 1e-06

def visible_index(packing):
    counts = jnp.transpose(packing[..., 1], (0, 2, 1)).astype(jnp.int32)
    offsets = jnp.transpose(packing[..., 0], (0, 2, 1)).astype(jnp.int32)
    ends = jnp.cumsum(counts, axis=-1).astype(jnp.int32)
    starts = (ends - counts).astype(jnp.int32)
    row_ids = jnp.arange(TOK_DEV, dtype=jnp.int32)
    source = lax.optimization_barrier(jnp.sum((row_ids[None, None, :, None] >= ends[:, :, None, :]).astype(jnp.int32), axis=-1)).astype(jnp.int32)
    picked = (source[..., None] == jnp.arange(N_SEQI, dtype=jnp.int32)).astype(jnp.int32)
    first_row = lax.optimization_barrier(jnp.sum(picked * starts[:, :, None, :], axis=-1)).astype(jnp.int32)
    anchor = lax.optimization_barrier(jnp.sum(picked * offsets[:, :, None, :], axis=-1)).astype(jnp.int32)
    groups = jnp.arange(N_SEQO, dtype=jnp.int32)[:, None, None]
    flat = (groups * N_SEQI + source) * TOK_DEV + anchor + row_ids[None, None, :] - first_row
    return flat.reshape(-1).astype(jnp.int32)

def block_mask(block_pattern):
    frames = jnp.arange(TOK_DEV, dtype=jnp.int32) // (TOK_DEV // NB)
    return block_pattern[frames][:, frames] > 0

def reference(loaded, packing, pattern, w_query, w_key, w_value, norm_gain, w_out):
    tokens = jnp.take(loaded, visible_index(packing), axis=0)
    query_rows = jnp.dot(tokens, w_query, preferred_element_type=jnp.float32).astype(jnp.bfloat16)
    key_rows = jnp.dot(tokens, w_key, preferred_element_type=jnp.float32).astype(jnp.bfloat16)
    value_rows = jnp.dot(tokens, w_value, preferred_element_type=jnp.float32).astype(jnp.bfloat16)
    query_rows = query_rows.reshape(SPANS, TOK_DEV, H, HD)
    key_rows = key_rows.reshape(SPANS, TOK_DEV, H, HD)
    value_rows = value_rows.reshape(SPANS, TOK_DEV, H, HD)

    def block_state(pair):
        return jnp.einsum('thd,the->hde', pair[0].astype(jnp.float32), pair[1].astype(jnp.float32), precision=lax.Precision.HIGHEST)
    states = lax.map(block_state, (key_rows, value_rows))
    running = jnp.cumsum(states, axis=0)
    prefix = jnp.concatenate([jnp.zeros_like(states[:1]), running[:-1]], axis=0)
    gain = norm_gain.astype(jnp.float32).reshape(H, HD)

    def block_output(items):
        query_block, key_block, value_block, block_pattern, carried_state = items
        scores = jnp.einsum('thd,shd->hts', query_block.astype(jnp.float32), key_block.astype(jnp.float32), precision=lax.Precision.HIGHEST)
        masked = jnp.where(block_mask(block_pattern)[None], scores, jnp.zeros_like(scores)).astype(jnp.bfloat16)
        local = jnp.einsum('hts,shd->thd', masked.astype(jnp.float32), value_block.astype(jnp.float32), precision=lax.Precision.HIGHEST)
        carried = jnp.einsum('thd,hde->the', query_block.astype(jnp.float32), carried_state, precision=lax.Precision.HIGHEST)
        attended = local + carried
        factor = lax.rsqrt(lax.optimization_barrier(jnp.mean(attended * attended, axis=-1, keepdims=True)) + EPSILON)
        normed = (attended * factor * gain).astype(jnp.bfloat16).reshape(TOK_DEV, D)
        return jnp.dot(normed, w_out, preferred_element_type=jnp.float32)
    outputs = lax.map(block_output, (query_rows, key_rows, value_rows, pattern, prefix))
    return outputs.reshape(SEQ, D)
```

```python
import functools

import jax
import jax.numpy as jnp
from jax import lax
from jax.experimental import pallas as pl
from jax.experimental.pallas import tpu as pltpu
from jax.sharding import PartitionSpec as P

H = 16
EPSILON = 1e-06
LANES = 256


F32 = jnp.float32
BF16 = jnp.bfloat16


def mm(a, b):
    return lax.dot_general(a, b, (((1,), (0,)), ((), ())), preferred_element_type=F32)


def mm_nt(a, b):
    return lax.dot_general(a, b, (((1,), (1,)), ((), ())), preferred_element_type=F32)


def mm_tn(a, b):
    return lax.dot_general(a, b, (((0,), (0,)), ((), ())), preferred_element_type=F32)


def iota(shape, dim):
    return lax.broadcasted_iota(jnp.int32, shape, dim)


def diagonal(blocks, head):
    width = blocks.shape[1]
    heads = width // head
    rows = blocks.shape[0] // heads
    column = iota((rows, width), 1) // head
    out = jnp.zeros((rows, width), blocks.dtype)
    for i in range(heads):
        out = jnp.where(column == i, blocks[i * rows : (i + 1) * rows], out)
    return out


def pack_kernel(axis, head, table, x_ref, wk_ref, wv_ref, *outs):
    n = len(outs) // 2
    slot_refs, s_ref, m_refs = outs[: n - 1], outs[n - 1], outs[n:]
    me = lax.axis_index(axis)
    rows = x_ref.shape[0]
    x = x_ref[...]
    key = mm(x, wk_ref[...]).astype(BF16)
    value = mm(x, wv_ref[...]).astype(BF16)
    row_id = iota(value.shape, 0)
    s_ref[...] = diagonal(mm_tn(key, value), head).astype(BF16)
    for k in range(n):
        bound = table[0, me, me ^ k, 0]
        kept = jnp.where(row_id < bound, value, jnp.zeros_like(value))
        m_refs[k][...] = diagonal(mm_tn(key, kept), head)
    cap = slot_refs[0].shape[0]
    width = wk_ref.shape[1]
    mine = x_ref[:, pl.ds(pl.multiple_of(pl.program_id(0) * width, width), width)]
    for k in range(1, n):
        first, count = table[0, me, me ^ k, 0], table[0, me, me ^ k, 1]
        slot, row = iota((cap, rows), 0), iota((cap, rows), 1)
        pick = jnp.logical_and(row == first + slot, slot < count)
        slot_refs[k - 1][...] = mm(pick.astype(BF16), mine).astype(BF16)


def local_kernel(axis, head, table, pattern_ref, x_ref, wq_ref, wk_ref, wv_ref, *rest):
    slots, (q_ref, local_ref, tokens) = rest[:-3], rest[-3:]
    n = len(slots) + 1
    rows = x_ref.shape[0]
    me = lax.axis_index(axis)

    @pl.when(pl.program_id(0) == 0)
    def _():
        total = None
        for k in range(n):
            source = me ^ k
            start = jnp.int32(0)
            for s in range(n):
                start += jnp.where(s < source, table[0, s, me, 1], 0)
            count = table[0, source, me, 1]
            held = x_ref[...] if k == 0 else slots[k - 1][...]
            first = table[0, me, me, 0] if k == 0 else 0
            row, slot = iota((rows, held.shape[0]), 0), iota((rows, held.shape[0]), 1)
            place = row - start
            pick = (slot == place + first) & (place >= 0) & (place < count)
            part = mm(pick.astype(BF16), held)
            total = part if total is None else total + part
        tokens[...] = total.astype(BF16)

    x = tokens[...]
    query = mm(x, wq_ref[...]).astype(BF16)
    key = mm(x, wk_ref[...]).astype(BF16)
    value = mm(x, wv_ref[...]).astype(BF16)
    width = query.shape[1]
    heads = width // head
    frames = pattern_ref.shape[1]
    per = rows // frames
    grow = (iota((rows, frames), 0) // per == iota((rows, frames), 1)).astype(BF16)
    seen = (pattern_ref[0] > 0).astype(BF16)
    allowed = mm_nt(mm(grow, seen).astype(BF16), grow) > 0.5
    column = iota((rows, width), 1) // head
    zero = jnp.zeros_like(query)
    stacked = jnp.concatenate([jnp.where(column == i, query, zero) for i in range(heads)], axis=0)
    scores = mm_nt(stacked, key)
    masked = jnp.concatenate(
        [jnp.where(allowed, scores[i * rows : (i + 1) * rows], 0.0) for i in range(heads)], axis=0
    ).astype(BF16)
    local_ref[...] = diagonal(mm(masked, value), head)
    q_ref[...] = query


def out_kernel(head, q_ref, local_ref, kept_ref, recv_ref, gain_ref, w_ref, out_ref):
    width = q_ref.shape[1]
    heads = width // head
    prefix = kept_ref[...] + recv_ref[...].astype(F32)
    same = iota((width, width), 0) // head == iota((width, width), 1) // head
    high = prefix.astype(BF16)
    low = (prefix - high.astype(F32)).astype(BF16)
    zero = jnp.zeros((width, width), BF16)
    query = q_ref[...]
    attended = local_ref[...]
    for part in (high, low):
        attended = attended + mm(query, jnp.where(same, jnp.concatenate([part] * heads, axis=0), zero))
    square = attended * attended
    sq_high = square.astype(BF16)
    sq_low = (square - sq_high.astype(F32)).astype(BF16)
    ones = same.astype(BF16)
    mean = (mm(sq_high, ones) + mm(sq_low, ones)) * (1.0 / head)
    normed = (attended * lax.rsqrt(mean + EPSILON) * gain_ref[...]).astype(BF16)
    piece = mm(normed, w_ref[...])

    @pl.when(pl.program_id(0) == 0)
    def _():
        out_ref[...] = piece

    @pl.when(pl.program_id(0) > 0)
    def _():
        out_ref[...] += piece


def swap(value, axis, bits):
    return lax.ppermute(value, axis, [(i, i ^ bits) for i in range(lax.axis_size(axis))])


def earlier_groups(state, axis):
    count, mine = lax.axis_size(axis), lax.axis_index(axis)
    before, total, stride = None, state, 1
    while stride < count:
        radix = min(4, count // stride)
        digit = (mine // stride) % radix
        came = [swap(total.astype(BF16), axis, k * stride).astype(F32) for k in range(1, radix)]
        for k, piece in enumerate(came, 1):
            piece_before = jnp.where((digit ^ k) < digit, piece, 0.0)
            before = piece_before if before is None else before + piece_before
        stride *= radix
        if stride < count:
            total = total.astype(F32) + sum(came)
    return before


def body(loaded, packing, pattern, w_query, w_key, w_value, norm_gain, w_out):
    n = lax.axis_size("seqi")
    rows, depth = loaded.shape
    head = depth // H
    width = min(LANES, depth)
    steps = depth // width
    cap = 2 * rows // n
    smem = pl.BlockSpec(memory_space=pltpu.SMEM)

    def whole(shape):
        return pl.BlockSpec(shape, lambda j: (0,) * len(shape))

    def columns(height):
        return pl.BlockSpec((height, width), lambda j: (0, j))

    packed = pl.pallas_call(
        functools.partial(pack_kernel, "seqi", head),
        grid=(steps,),
        in_specs=[smem, whole((rows, depth)), columns(depth), columns(depth)],
        out_specs=[columns(cap)] * (n - 1) + [columns(head)] * (n + 1),
        out_shape=[jax.ShapeDtypeStruct((cap, depth), BF16)] * (n - 1)
        + [jax.ShapeDtypeStruct((head, depth), BF16)]
        + [jax.ShapeDtypeStruct((head, depth), F32)] * n,
        cost_estimate=pl.CostEstimate(
            flops=4 * rows * depth * depth, bytes_accessed=4 * depth * depth, transcendentals=0
        ),
        name="pack",
    )(packing, loaded, w_key, w_value)
    slots, state, bound = packed[: n - 1], packed[n - 1], packed[n:]

    before = earlier_groups(state, "seqo")
    came = [swap(slots[k - 1], "seqi", k) for k in range(1, n)]

    held = {k: bound[k] if before is None else before + bound[k] for k in range(n)}
    bit = 1
    while bit < n:
        send = [k for k in held if k & bit]
        if 2 * bit < n or len(send) > 1:
            got = swap(jnp.stack([held[k].astype(BF16) for k in send]), "seqi", bit)
            got = [got[i] for i in range(len(send))]
        else:
            got = [swap(held[send[0]].astype(BF16), "seqi", bit)]
        if 2 * bit < n:
            held = {k ^ bit: held[k ^ bit] + g.astype(F32) for k, g in zip(send, got)}
        else:
            last = got[0]
        bit *= 2

    query, local = pl.pallas_call(
        functools.partial(local_kernel, "seqi", head),
        grid=(steps,),
        in_specs=[smem, whole(pattern.shape), whole((rows, depth))]
        + [columns(depth)] * 3
        + [whole((cap, depth))] * (n - 1),
        out_specs=[columns(rows), columns(rows)],
        out_shape=[
            jax.ShapeDtypeStruct((rows, depth), BF16),
            jax.ShapeDtypeStruct((rows, depth), F32),
        ],
        scratch_shapes=[pltpu.VMEM((rows, depth), BF16)],
        cost_estimate=pl.CostEstimate(
            flops=6 * rows * depth * depth, bytes_accessed=6 * depth * depth, transcendentals=0
        ),
        name="local",
    )(packing, pattern, loaded, w_query, w_key, w_value, *came)

    return pl.pallas_call(
        functools.partial(out_kernel, head),
        grid=(steps,),
        in_specs=[
            columns(rows),
            columns(rows),
            columns(head),
            columns(head),
            columns(1),
            pl.BlockSpec((width, depth), lambda j: (j, 0)),
        ],
        out_specs=whole((rows, depth)),
        out_shape=jax.ShapeDtypeStruct((rows, depth), F32),
        cost_estimate=pl.CostEstimate(
            flops=2 * rows * depth * depth, bytes_accessed=2 * depth * depth, transcendentals=0
        ),
        name="out",
    )(query, local, held[0], last, norm_gain.reshape(1, depth), w_out)


def solution(mesh):
    return jax.shard_map(
        body,
        mesh=mesh,
        in_specs=(
            P(("dp", "seqo", "seqi"), None),
            P(("dp", "seqo"), None, None, None),
            P(("dp", "seqo", "seqi"), None, None),
            P(),
            P(),
            P(),
            P(),
            P(),
        ),
        out_specs=P(("dp", "seqo", "seqi"), None),
        check_vma=False,
    )
```

```python
import functools

import jax
import jax.numpy as jnp
from jax import lax
from jax.experimental import pallas as pl
from jax.experimental.pallas import tpu as pltpu
from jax.sharding import PartitionSpec as P


H = 16
EPSILON = 1e-06
LANES = 256
VMEM = 16 * 2**20


F32 = jnp.float32
BF16 = jnp.bfloat16


def mm(a, b):
    return lax.dot_general(a, b, (((1,), (0,)), ((), ())), preferred_element_type=F32)


def mm_nt(a, b):
    return lax.dot_general(a, b, (((1,), (1,)), ((), ())), preferred_element_type=F32)


def mm_tn(a, b):
    return lax.dot_general(a, b, (((0,), (0,)), ((), ())), preferred_element_type=F32)


def iota(shape, dim):
    return lax.broadcasted_iota(jnp.int32, shape, dim)


def diagonal(blocks, head):
    width = blocks.shape[1]
    heads = width // head
    rows = blocks.shape[0] // heads
    column = iota((rows, width), 1) // head
    out = jnp.zeros((rows, width), blocks.dtype)
    for i in range(heads):
        out = jnp.where(column == i, blocks[i * rows : (i + 1) * rows], out)
    return out


def fetch(pairs, sems):
    copies = [pltpu.make_async_copy(src, dst, sems.at[i]) for i, (src, dst) in enumerate(pairs)]
    for copy in copies:
        copy.start()
    return copies


def state_kernel(head, width, x_hbm, wk_hbm, wv_hbm, s_ref, key_ref, value_ref, x, wk, wv, sems):
    steps = x.shape[1] // width
    pairs = [(x_hbm, x)]
    for j in range(steps):
        cols = pl.ds(j * width, width)
        pairs += [(wk_hbm.at[:, cols], wk.at[:, cols]), (wv_hbm.at[:, cols], wv.at[:, cols])]
    copies = fetch(pairs, sems)
    copies[0].wait()
    rows = x[...]
    for j in range(steps):
        cols = pl.ds(j * width, width)
        copies[1 + 2 * j].wait()
        key = mm(rows, wk[:, cols]).astype(BF16)
        copies[2 + 2 * j].wait()
        value = mm(rows, wv[:, cols]).astype(BF16)
        key_ref[:, cols], value_ref[:, cols] = key, value
        s_ref[:, cols] = diagonal(mm_tn(key, value), head).astype(BF16)


def slot_kernel(axis, table, x_ref, *slot_refs):
    me = lax.axis_index(axis)
    rows, cap = x_ref.shape[0], slot_refs[0].shape[0]
    x = x_ref[...]
    slot, row = iota((cap, rows), 0), iota((cap, rows), 1)
    for k, slot_ref in enumerate(slot_refs, 1):
        first, count = table[0, me, 0, me ^ k], table[0, me, 1, me ^ k]
        pick = jnp.logical_and(row == first + slot, slot < count)
        slot_ref[...] = mm(pick.astype(BF16), x).astype(BF16)


def bound_kernel(axis, head, width, table, key_ref, value_ref, *m_refs):
    me = lax.axis_index(axis)
    rows, depth = key_ref.shape
    row = iota((rows, width), 0)
    for j in range(depth // width):
        cols = pl.ds(j * width, width)
        key, value = key_ref[:, cols], value_ref[:, cols]
        for k, m_ref in enumerate(m_refs):
            kept = jnp.where(row < table[0, me, 0, me ^ k], value, jnp.zeros_like(value))
            m_ref[:, cols] = diagonal(mm_tn(key, kept), head)


def local_kernel(axis, head, width, table, pattern_ref, x_ref, wq_hbm, wk_hbm, wv_hbm, *rest):
    slots, (q_ref, local_ref, wq, wk, wv, sems) = rest[:-6], rest[-6:]
    rows, depth = x_ref.shape
    n, steps = len(slots) + 1, depth // width
    pairs = []
    for j in range(steps):
        cols = pl.ds(j * width, width)
        for src, dst in ((wq_hbm, wq), (wk_hbm, wk), (wv_hbm, wv)):
            pairs.append((src.at[:, cols], dst.at[:, cols]))
    copies = fetch(pairs, sems)
    me = lax.axis_index(axis)
    total = None
    for k in range(n):
        source = me ^ k
        start = jnp.int32(0)
        for s in range(n):
            start += jnp.where(s < source, table[0, s, 1, me], 0)
        count = table[0, source, 1, me]
        held = x_ref[...] if k == 0 else slots[k - 1][...]
        first = table[0, me, 0, me] if k == 0 else 0
        row, slot = iota((rows, held.shape[0]), 0), iota((rows, held.shape[0]), 1)
        place = row - start
        pick = (slot == place + first) & (place >= 0) & (place < count)
        part = mm(pick.astype(BF16), held)
        total = part if total is None else total + part
    x = total.astype(BF16)
    frames = pattern_ref.shape[1]
    per = rows // frames
    grow = (iota((rows, frames), 0) // per == iota((rows, frames), 1)).astype(BF16)
    seen = (pattern_ref[0] > 0).astype(BF16)
    allowed = mm_nt(mm(grow, seen).astype(BF16), grow) > 0.5
    heads = width // head
    column = iota((rows, width), 1) // head
    for j in range(steps):
        cols = pl.ds(j * width, width)
        copies[3 * j].wait()
        query = mm(x, wq[:, cols]).astype(BF16)
        copies[3 * j + 1].wait()
        key = mm(x, wk[:, cols]).astype(BF16)
        copies[3 * j + 2].wait()
        value = mm(x, wv[:, cols]).astype(BF16)
        zero = jnp.zeros_like(query)
        stacked = jnp.concatenate([jnp.where(column == i, query, zero) for i in range(heads)], axis=0)
        scores = mm_nt(stacked, key)
        masked = jnp.concatenate(
            [jnp.where(allowed, scores[i * rows : (i + 1) * rows], 0.0) for i in range(heads)], axis=0
        ).astype(BF16)
        local_ref[:, cols] = diagonal(mm(masked, value), head)
        q_ref[:, cols] = query


def out_kernel(head, width, q_ref, local_ref, kept_ref, recv_ref, gain_ref, w_hbm, out_ref, w, sems):
    _, depth = q_ref.shape
    steps = depth // width
    pairs = []
    for j in range(steps):
        part = pl.ds(j * width, width)
        pairs.append((w_hbm.at[part], w.at[part]))
    copies = fetch(pairs, sems)
    heads = width // head
    same = iota((width, width), 0) // head == iota((width, width), 1) // head
    ones = same.astype(BF16)
    zero = jnp.zeros((width, width), BF16)
    total = None
    for j in range(steps):
        cols = pl.ds(j * width, width)
        prefix = kept_ref[:, cols] + recv_ref[:, cols].astype(F32)
        high = prefix.astype(BF16)
        low = (prefix - high.astype(F32)).astype(BF16)
        query = q_ref[:, cols]
        attended = local_ref[:, cols]
        for part in (high, low):
            spread = jnp.where(same, jnp.concatenate([part] * heads, axis=0), zero)
            attended = attended + mm(query, spread)
        square = attended * attended
        sq_high = square.astype(BF16)
        sq_low = (square - sq_high.astype(F32)).astype(BF16)
        mean = (mm(sq_high, ones) + mm(sq_low, ones)) * (1.0 / head)
        normed = (attended * lax.rsqrt(mean + EPSILON) * gain_ref[:, cols]).astype(BF16)
        copies[j].wait()
        piece = mm(normed, w[pl.ds(j * width, width), :])
        total = piece if total is None else total + piece
    out_ref[...] = total


def swap(value, axis, bits):
    return lax.ppermute(value, axis, [(i, i ^ bits) for i in range(lax.axis_size(axis))])


def earlier_groups(state, axis):
    count, mine = lax.axis_size(axis), lax.axis_index(axis)
    before, total, stride = None, state, 1
    while stride < count:
        radix = min(4, count // stride)
        digit = (mine // stride) % radix
        came = [swap(total.astype(BF16), axis, k * stride).astype(F32) for k in range(1, radix)]
        for k, piece in enumerate(came, 1):
            piece_before = jnp.where((digit ^ k) < digit, piece, 0.0)
            before = piece_before if before is None else before + piece_before
        stride *= radix
        if stride < count:
            total = total.astype(F32) + sum(came)
    return before


def cost(flops, size):
    return pl.CostEstimate(flops=flops, bytes_accessed=size, transcendentals=0)


def body(loaded, packing, pattern, w_query, w_key, w_value, norm_gain, w_out):
    n = lax.axis_size("seqi")
    rows, depth = loaded.shape
    head = depth // H
    width = min(LANES, depth)
    steps = depth // width
    cap = 2 * rows // n
    square = depth * depth
    table = jnp.swapaxes(packing, 2, 3)
    smem = pl.BlockSpec(memory_space=pltpu.SMEM)
    vmem = pl.BlockSpec(memory_space=pltpu.VMEM)
    hbm = pl.BlockSpec(memory_space=pltpu.HBM)
    shape = jax.ShapeDtypeStruct
    weight = pltpu.VMEM((depth, depth), BF16)
    params = pltpu.CompilerParams(vmem_limit_bytes=VMEM)

    state, key, value = pl.pallas_call(
        functools.partial(state_kernel, head, width),
        in_specs=[hbm] * 3,
        out_specs=[vmem] * 3,
        out_shape=[shape((head, depth), BF16)] + [shape((rows, depth), BF16)] * 2,
        scratch_shapes=[pltpu.VMEM((rows, depth), BF16), weight, weight]
        + [pltpu.SemaphoreType.DMA((1 + 2 * steps,))],
        cost_estimate=cost(4 * rows * square, 4 * square),
        name="states",
    )(loaded, w_key, w_value)
    before = earlier_groups(state, "seqo")
    slots = pl.pallas_call(
        functools.partial(slot_kernel, "seqi"),
        in_specs=[smem, vmem],
        out_specs=[vmem] * (n - 1),
        out_shape=[shape((cap, depth), BF16)] * (n - 1),
        compiler_params=params,
        cost_estimate=cost(4 * rows * rows * depth, 4 * rows * depth),
        name="slots",
    )(table, loaded)
    came = [swap(slots[k - 1], "seqi", k) for k in range(1, n)]
    bound = pl.pallas_call(
        functools.partial(bound_kernel, "seqi", head, width),
        in_specs=[smem, vmem, vmem],
        out_specs=[vmem] * n,
        out_shape=[shape((head, depth), F32)] * n,
        compiler_params=params,
        cost_estimate=cost(2 * n * rows * head * depth * 4, 4 * rows * depth),
        name="bounds",
    )(table, key, value)

    held = {k: bound[k] if before is None else before + bound[k] for k in range(n)}
    bit = 1
    while bit < n:
        send = [k for k in held if k & bit]
        if len(send) > 1:
            got = swap(jnp.stack([held[k].astype(BF16) for k in send]), "seqi", bit)
        else:
            got = [swap(held[send[0]].astype(BF16), "seqi", bit)]
        if 2 * bit < n:
            held = {k ^ bit: held[k ^ bit] + got[i].astype(F32) for i, k in enumerate(send)}
        else:
            last = got[0]
        bit *= 2

    query, local = pl.pallas_call(
        functools.partial(local_kernel, "seqi", head, width),
        in_specs=[smem, vmem, vmem] + [hbm] * 3 + [vmem] * (n - 1),
        out_specs=[vmem] * 2,
        out_shape=[shape((rows, depth), BF16), shape((rows, depth), F32)],
        scratch_shapes=[weight] * 3 + [pltpu.SemaphoreType.DMA((3 * steps,))],
        compiler_params=params,
        cost_estimate=cost(6 * rows * square, 6 * square),
        name="local",
    )(table, pattern, loaded, w_query, w_key, w_value, *came)

    return pl.pallas_call(
        functools.partial(out_kernel, head, width),
        in_specs=[vmem] * 5 + [hbm],
        out_specs=vmem,
        out_shape=shape((rows, depth), F32),
        scratch_shapes=[weight, pltpu.SemaphoreType.DMA((steps,))],
        compiler_params=params,
        cost_estimate=cost(2 * rows * square, 2 * square),
        name="out",
    )(query, local, held[0], last, norm_gain.reshape(1, depth), w_out)


def solution(mesh):
    return jax.shard_map(
        body,
        mesh=mesh,
        in_specs=(
            P(("dp", "seqo", "seqi"), None),
            P(("dp", "seqo"), None, None, None),
            P(("dp", "seqo", "seqi"), None, None),
            P(),
            P(),
            P(),
            P(),
            P(),
        ),
        out_specs=P(("dp", "seqo", "seqi"), None),
        check_vma=False,
    )
```

```python
import functools

import jax
import jax.numpy as jnp
from jax import lax
from jax.experimental import pallas as pl
from jax.experimental.pallas import tpu as pltpu
from jax.sharding import PartitionSpec as P


H = 16
EPSILON = 1e-06
LANES = 256
VMEM = 16 * 2**20
SLOTS_COST = 10**11
CHUNKS = 2


F32 = jnp.float32
BF16 = jnp.bfloat16


def mm(a, b):
    return lax.dot_general(a, b, (((1,), (0,)), ((), ())), preferred_element_type=F32)


def mm_nt(a, b):
    return lax.dot_general(a, b, (((1,), (1,)), ((), ())), preferred_element_type=F32)


def mm_tn(a, b):
    return lax.dot_general(a, b, (((0,), (0,)), ((), ())), preferred_element_type=F32)


def iota(shape, dim):
    return lax.broadcasted_iota(jnp.int32, shape, dim)


def diagonal(blocks, head):
    width = blocks.shape[1]
    heads = width // head
    rows = blocks.shape[0] // heads
    column = iota((rows, width), 1) // head
    out = jnp.zeros((rows, width), blocks.dtype)
    for i in range(heads):
        out = jnp.where(column == i, blocks[i * rows : (i + 1) * rows], out)
    return out


def state_kernel(head, width, x_ref, wk, wv, s_ref, key_ref, value_ref):
    rows = x_ref[...]
    for j in range(rows.shape[1] // width):
        cols = pl.ds(j * width, width)
        key = mm(rows, wk[:, cols]).astype(BF16)
        value = mm(rows, wv[:, cols]).astype(BF16)
        key_ref[:, cols], value_ref[:, cols] = key, value
        s_ref[:, cols] = diagonal(mm_tn(key, value), head).astype(BF16)


def slot_kernel(axis, table, x_ref, *slot_refs):
    me = lax.axis_index(axis)
    rows, cap = x_ref.shape[0], slot_refs[0].shape[0]
    x = x_ref[...]
    slot, row = iota((cap, rows), 0), iota((cap, rows), 1)
    for k, slot_ref in enumerate(slot_refs, 1):
        first, count = table[0, me, 0, me ^ k], table[0, me, 1, me ^ k]
        pick = jnp.logical_and(row == first + slot, slot < count)
        slot_ref[...] = mm(pick.astype(BF16), x).astype(BF16)


def bound_kernel(axis, head, width, table, key_ref, value_ref, *m_refs):
    me = lax.axis_index(axis)
    rows, depth = key_ref.shape
    row = iota((rows, width), 0)
    for j in range(depth // width):
        cols = pl.ds(j * width, width)
        key, value = key_ref[:, cols], value_ref[:, cols]
        for k, m_ref in enumerate(m_refs):
            kept = jnp.where(row < table[0, me, 0, me ^ k], value, jnp.zeros_like(value))
            m_ref[:, cols] = diagonal(mm_tn(key, kept), head)


def local_kernel(axis, head, width, table, pattern_ref, x_ref, wq, wk, wv, *rest):
    slots, (q_ref, local_ref) = rest[:-2], rest[-2:]
    rows, depth = x_ref.shape
    n, steps = len(slots) + 1, depth // width
    me = lax.axis_index(axis)
    total = None
    for k in range(n):
        source = me ^ k
        start = jnp.int32(0)
        for s in range(n):
            start += jnp.where(s < source, table[0, s, 1, me], 0)
        count = table[0, source, 1, me]
        held = x_ref[...] if k == 0 else slots[k - 1][...]
        first = table[0, me, 0, me] if k == 0 else 0
        row, slot = iota((rows, held.shape[0]), 0), iota((rows, held.shape[0]), 1)
        place = row - start
        pick = (slot == place + first) & (place >= 0) & (place < count)
        part = mm(pick.astype(BF16), held)
        total = part if total is None else total + part
    x = total.astype(BF16)
    frames = pattern_ref.shape[1]
    per = rows // frames
    grow = (iota((rows, frames), 0) // per == iota((rows, frames), 1)).astype(BF16)
    seen = (pattern_ref[0] > 0).astype(BF16)
    allowed = mm_nt(mm(grow, seen).astype(BF16), grow) > 0.5
    heads = width // head
    column = iota((rows, width), 1) // head
    for j in range(steps):
        cols = pl.ds(j * width, width)
        query = mm(x, wq[:, cols]).astype(BF16)
        key = mm(x, wk[:, cols]).astype(BF16)
        value = mm(x, wv[:, cols]).astype(BF16)
        zero = jnp.zeros_like(query)
        stacked = jnp.concatenate([jnp.where(column == i, query, zero) for i in range(heads)], axis=0)
        scores = mm_nt(stacked, key)
        masked = jnp.concatenate(
            [jnp.where(allowed, scores[i * rows : (i + 1) * rows], 0.0) for i in range(heads)], axis=0
        ).astype(BF16)
        local_ref[:, cols] = diagonal(mm(masked, value), head)
        q_ref[:, cols] = query


def out_kernel(head, width, q_ref, local_ref, *rest):
    kept_refs, recv_refs, (gain_ref, w, out_ref) = rest[:CHUNKS], rest[CHUNKS:-3], rest[-3:]
    _, depth = q_ref.shape
    steps = depth // width
    heads = width // head
    same = iota((width, width), 0) // head == iota((width, width), 1) // head
    ones = same.astype(BF16)
    zero = jnp.zeros((width, width), BF16)
    total = None
    for j in range(steps):
        cols = pl.ds(j * width, width)
        chunk, place = divmod(j * width, depth // CHUNKS)
        inner = pl.ds(place, width)
        prefix = kept_refs[chunk][:, inner] + recv_refs[chunk][:, inner].astype(F32)
        high = prefix.astype(BF16)
        low = (prefix - high.astype(F32)).astype(BF16)
        query = q_ref[:, cols]
        attended = local_ref[:, cols]
        for part in (high, low):
            spread = jnp.where(same, jnp.concatenate([part] * heads, axis=0), zero)
            attended = attended + mm(query, spread)
        square = attended * attended
        sq_high = square.astype(BF16)
        sq_low = (square - sq_high.astype(F32)).astype(BF16)
        mean = (mm(sq_high, ones) + mm(sq_low, ones)) * (1.0 / head)
        normed = (attended * lax.rsqrt(mean + EPSILON) * gain_ref[:, cols]).astype(BF16)
        piece = mm(normed, w[pl.ds(j * width, width), :])
        total = piece if total is None else total + piece
    out_ref[...] = total


def swap(value, axis, bits):
    return lax.ppermute(value, axis, [(i, i ^ bits) for i in range(lax.axis_size(axis))])


def earlier_groups(state, axis):
    count, mine = lax.axis_size(axis), lax.axis_index(axis)
    before, total, stride = None, state, 1
    while True:
        radix = min(4, count // stride)
        came = [swap(total.astype(BF16), axis, k * stride) for k in range(1, radix)]
        if stride * radix >= count:
            return before, came, stride
        digit = (mine // stride) % radix
        wide = [piece.astype(F32) for piece in came]
        for k, piece in enumerate(wide, 1):
            piece_before = jnp.where((digit ^ k) < digit, piece, 0.0)
            before = piece_before if before is None else before + piece_before
        total = total.astype(F32) + sum(wide)
        stride *= radix


def merge_kernel(axis, stride, n, *refs):
    outs = 2 * CHUNKS
    ins, (send_refs, keep_refs) = refs[:-outs], (refs[-outs:][:CHUNKS], refs[-CHUNKS:])
    bound_refs, came_refs = ins[:n], ins[n:]
    extra = len(came_refs) & 1 ^ 1
    base_ref, came_refs = (came_refs[0], came_refs[1:]) if extra else (None, came_refs)
    digit = (lax.axis_index(axis) // stride) % (len(came_refs) + 1)
    width = send_refs[0].shape[2]
    for c in range(CHUNKS):
        cols = pl.ds(c * width, width)
        early = None if base_ref is None else base_ref[:, cols]
        for k, came_ref in enumerate(came_refs, 1):
            piece = jnp.where((digit ^ k) < digit, came_ref[:, cols].astype(F32), 0.0)
            early = piece if early is None else early + piece
        for k in range(n):
            held = early + bound_refs[k][:, cols]
            if k & 1:
                send_refs[c][k // 2] = held.astype(BF16)
            else:
                keep_refs[c][k // 2] = held


def near(value):
    return pltpu.with_memory_space_constraint(value, pltpu.VMEM)


def far(value):
    return pltpu.with_memory_space_constraint(value, pltpu.HBM)


def merged(held, got, bit):
    kept = [k for k in held if not k & bit]
    return {k: held[k] + got[i].astype(F32) for i, k in enumerate(kept)}


def cost(flops, size):
    return pl.CostEstimate(flops=flops, bytes_accessed=size, transcendentals=0)


def body(loaded, packing, pattern, w_query, w_key, w_value, norm_gain, w_out):
    n = lax.axis_size("seqi")
    rows, depth = loaded.shape
    head = depth // H
    width = min(LANES, depth)
    cap = 2 * rows // n
    square = depth * depth
    table = jnp.swapaxes(packing, 2, 3)
    smem = pl.BlockSpec(memory_space=pltpu.SMEM)
    vmem = pl.BlockSpec(memory_space=pltpu.VMEM)
    hbm = pl.BlockSpec(memory_space=pltpu.HBM)
    shape = jax.ShapeDtypeStruct
    weight = pltpu.VMEM((depth, depth), BF16)
    params = pltpu.CompilerParams(vmem_limit_bytes=VMEM)

    slots = pl.pallas_call(
        functools.partial(slot_kernel, "seqi"),
        in_specs=[smem, vmem],
        out_specs=[vmem] * (n - 1),
        out_shape=[pltpu.VMEM((cap, depth), BF16)] * (n - 1),
        compiler_params=params,
        cost_estimate=cost(SLOTS_COST, 4 * rows * depth),
        name="slots",
    )(far(table), far(loaded))
    came = [swap(slots[k - 1], "seqi", k) for k in range(1, n)]
    state, key, value = pl.pallas_call(
        functools.partial(state_kernel, head, width),
        in_specs=[vmem] * 3,
        out_specs=[vmem] * 3,
        out_shape=[pltpu.VMEM((head, depth), BF16)] + [pltpu.VMEM((rows, depth), BF16)] * 2,
        compiler_params=params,
        cost_estimate=cost(4 * rows * square, 4 * square),
        name="states",
    )(loaded, w_key, w_value)
    before, groups, stride = earlier_groups(state, "seqo")
    bound = pl.pallas_call(
        functools.partial(bound_kernel, "seqi", head, width),
        in_specs=[smem, vmem, vmem],
        out_specs=[vmem] * n,
        out_shape=[shape((head, depth), F32)] * n,
        compiler_params=params,
        cost_estimate=cost(2 * n * rows * head * depth * 4, 4 * rows * depth),
        name="bounds",
    )(table, key, value)

    chunk = depth // CHUNKS
    earlier = ([] if before is None else [before]) + groups
    merge = pl.pallas_call(
        functools.partial(merge_kernel, "seqo", stride, n),
        in_specs=[vmem] * (n + len(earlier)),
        out_specs=[vmem] * (2 * CHUNKS),
        out_shape=[pltpu.VMEM((n // 2, head, chunk), BF16)] * CHUNKS
        + [pltpu.VMEM((n // 2, head, chunk), F32)] * CHUNKS,
        compiler_params=params,
        cost_estimate=cost(2 * n * head * depth, 8 * n * head * depth),
        name="merge",
    )(*bound, *(near(piece) for piece in earlier))
    parts, gate = [], None
    for c in range(CHUNKS):
        got = swap(merge[c], "seqi", 1)
        parts.append(({k: merge[CHUNKS + c][k // 2] for k in range(0, n, 2)}, got))
    bit = 2
    while bit < n:
        for c, (held, got) in enumerate(parts):
            if c > 0:
                got, _ = lax.optimization_barrier((got, gate))
            held = merged(held, got, bit // 2)
            send = [held[k].astype(BF16) for k in held if k & bit]
            gate = jnp.stack(send) if len(send) > 1 else send[0][None]
            parts[c] = held, swap(gate, "seqi", bit)
        bit *= 2
    kept, last = [held[0] for held, _ in parts], [got[0] for _, got in parts]

    query, local = pl.pallas_call(
        functools.partial(local_kernel, "seqi", head, width),
        in_specs=[smem] + [vmem] * (n + 4),
        out_specs=[vmem] * 2,
        out_shape=[shape((rows, depth), BF16), shape((rows, depth), F32)],
        compiler_params=params,
        cost_estimate=cost(6 * rows * square, 6 * square),
        name="local",
    )(table, pattern, loaded, w_query, w_key, w_value, *came)

    return pl.pallas_call(
        functools.partial(out_kernel, head, width),
        in_specs=[vmem] * (4 + 2 * CHUNKS),
        out_specs=vmem,
        out_shape=shape((rows, depth), F32),
        compiler_params=params,
        cost_estimate=cost(2 * rows * square, 2 * square),
        name="out",
    )(query, local, *kept, *last, norm_gain.reshape(1, depth), w_out)


def solution(mesh):
    return jax.shard_map(
        body,
        mesh=mesh,
        in_specs=(
            P(("dp", "seqo", "seqi"), None),
            P(("dp", "seqo"), None, None, None),
            P(("dp", "seqo", "seqi"), None, None),
            P(),
            P(),
            P(),
            P(),
            P(),
        ),
        out_specs=P(("dp", "seqo", "seqi"), None),
        check_vma=False,
    )
```

```python
import functools

import jax
import jax.numpy as jnp
from jax import lax
from jax.experimental import pallas as pl
from jax.experimental.pallas import tpu as pltpu
from jax.sharding import PartitionSpec as P


H = 16
EPSILON = 1e-06
LANES = 256
VMEM = 16 * 2**20
SLOTS_COST = 10**11
CHUNKS = 2


F32 = jnp.float32
BF16 = jnp.bfloat16


def mm(a, b):
    return lax.dot_general(a, b, (((1,), (0,)), ((), ())), preferred_element_type=F32)


def mm_nt(a, b):
    return lax.dot_general(a, b, (((1,), (1,)), ((), ())), preferred_element_type=F32)


def mm_tn(a, b):
    return lax.dot_general(a, b, (((0,), (0,)), ((), ())), preferred_element_type=F32)


def iota(shape, dim):
    return lax.broadcasted_iota(jnp.int32, shape, dim)


def diagonal(blocks, head):
    width = blocks.shape[1]
    heads = width // head
    rows = blocks.shape[0] // heads
    column = iota((rows, width), 1) // head
    out = jnp.zeros((rows, width), blocks.dtype)
    for i in range(heads):
        out = jnp.where(column == i, blocks[i * rows : (i + 1) * rows], out)
    return out


def state_kernel(head, width, x_ref, wk, wv, key_ref, value_ref, s_ref):
    rows = x_ref[...]
    for j in range(rows.shape[1] // width):
        cols = pl.ds(j * width, width)
        key = mm(rows, wk[:, cols]).astype(BF16)
        value = mm(rows, wv[:, cols]).astype(BF16)
        key_ref[:, cols], value_ref[:, cols] = key, value
        s_ref[:, cols] = diagonal(mm_tn(key, value), head).astype(BF16)


def slot_kernel(axis, table, x_ref, *slot_refs):
    me = lax.axis_index(axis)
    rows, cap = x_ref.shape[0], slot_refs[0].shape[0]
    x = x_ref[...]
    slot, row = iota((cap, rows), 0), iota((cap, rows), 1)
    for k, slot_ref in enumerate(slot_refs, 1):
        first, count = table[0, me, 0, me ^ k], table[0, me, 1, me ^ k]
        pick = jnp.logical_and(row == first + slot, slot < count)
        slot_ref[...] = mm(pick.astype(BF16), x).astype(BF16)


def bound_kernel(axis, head, width, table, key_ref, value_ref, *m_refs):
    me = lax.axis_index(axis)
    rows, depth = key_ref.shape
    row = iota((rows, width), 0)
    for j in range(depth // width):
        cols = pl.ds(j * width, width)
        key, value = key_ref[:, cols], value_ref[:, cols]
        for k, m_ref in enumerate(m_refs):
            kept = jnp.where(row < table[0, me, 0, me ^ k], value, jnp.zeros_like(value))
            m_ref[:, cols] = diagonal(mm_tn(key, kept), head)


def unpack(axis, table, x_ref, slots):
    rows, me = x_ref.shape[0], lax.axis_index(axis)
    total = None
    for k, held_ref in enumerate((x_ref, *slots)):
        source = me ^ k
        start = jnp.int32(0)
        for s in range(len(slots) + 1):
            start += jnp.where(s < source, table[0, s, 1, me], 0)
        count = table[0, source, 1, me]
        held = held_ref[...]
        first = table[0, me, 0, me] if k == 0 else 0
        row, slot = iota((rows, held.shape[0]), 0), iota((rows, held.shape[0]), 1)
        place = row - start
        pick = (slot == place + first) & (place >= 0) & (place < count)
        part = mm(pick.astype(BF16), held)
        total = part if total is None else total + part
    return total.astype(BF16)


def local_kernel(axis, head, width, place, *refs):
    if place == 0:
        (table, pattern_ref, x_ref, wq, wk, wv, *slots), (q_ref, local_ref, tokens_ref) = refs[:-3], refs[-3:]
        x = unpack(axis, table, x_ref, slots)
        tokens_ref[...] = x
    else:
        pattern_ref, tokens_ref, wq, wk, wv, q_ref, local_ref = refs
        x = tokens_ref[...]
    rows = x.shape[0]
    frames = pattern_ref.shape[1]
    per = rows // frames
    grow = (iota((rows, frames), 0) // per == iota((rows, frames), 1)).astype(BF16)
    seen = (pattern_ref[0] > 0).astype(BF16)
    allowed = mm_nt(mm(grow, seen).astype(BF16), grow) > 0.5
    heads = width // head
    column = iota((rows, width), 1) // head
    for j in range(q_ref.shape[1] // width):
        inner, cols = pl.ds(j * width, width), pl.ds(place + j * width, width)
        query = mm(x, wq[:, cols]).astype(BF16)
        key = mm(x, wk[:, cols]).astype(BF16)
        value = mm(x, wv[:, cols]).astype(BF16)
        zero = jnp.zeros_like(query)
        stacked = jnp.concatenate([jnp.where(column == i, query, zero) for i in range(heads)], axis=0)
        scores = mm_nt(stacked, key)
        masked = jnp.concatenate(
            [jnp.where(allowed, scores[i * rows : (i + 1) * rows], 0.0) for i in range(heads)], axis=0
        ).astype(BF16)
        local_ref[:, inner] = diagonal(mm(masked, value), head)
        q_ref[:, inner] = query


def out_kernel(head, width, place, depth, q_ref, local_ref, kept_ref, recv_ref, gain_ref, w, *rest):
    chunk = kept_ref.shape[1]
    so_far, rest = (rest[0], rest[1:]) if place > 0 else (None, rest)
    heads = width // head
    same = iota((width, width), 0) // head == iota((width, width), 1) // head
    ones = same.astype(BF16)
    zero = jnp.zeros((width, width), BF16)
    normed = []
    for j in range(chunk // width):
        inner, cols = pl.ds(j * width, width), pl.ds(place + j * width, width)
        prefix = kept_ref[:, inner] + recv_ref[:, inner].astype(F32)
        high = prefix.astype(BF16)
        low = (prefix - high.astype(F32)).astype(BF16)
        query = q_ref[:, inner]
        attended = local_ref[:, inner]
        for part in (high, low):
            spread = jnp.where(same, jnp.concatenate([part] * heads, axis=0), zero)
            attended = attended + mm(query, spread)
        square = attended * attended
        sq_high = square.astype(BF16)
        sq_low = (square - sq_high.astype(F32)).astype(BF16)
        mean = (mm(sq_high, ones) + mm(sq_low, ones)) * (1.0 / head)
        normed.append((attended * lax.rsqrt(mean + EPSILON) * gain_ref[:, cols]).astype(BF16))
    normed = jnp.concatenate(normed, axis=1)
    copies = []
    for j in range(depth // width):
        cols = pl.ds(j * width, width)
        piece = mm(normed, w[pl.ds(place, chunk), cols])
        piece = piece if so_far is None else so_far[:, cols] + piece
        if place + chunk < depth:
            rest[0][:, cols] = piece
        else:
            out_hbm, total, sems = rest
            total[:, cols] = piece
            copies.append(pltpu.make_async_copy(total.at[:, cols], out_hbm.at[:, cols], sems.at[j]))
            copies[j].start()
    for copy in copies:
        copy.wait()


def swap(value, axis, bits):
    return lax.ppermute(value, axis, [(i, i ^ bits) for i in range(lax.axis_size(axis))])


def earlier_groups(state, axis):
    count, mine = lax.axis_size(axis), lax.axis_index(axis)
    before, total, stride = None, state, 1
    while True:
        radix = min(4, count // stride)
        came = [swap(total.astype(BF16), axis, k * stride) for k in range(1, radix)]
        if stride * radix >= count:
            return before, came, stride
        digit = (mine // stride) % radix
        wide = [piece.astype(F32) for piece in came]
        for k, piece in enumerate(wide, 1):
            piece_before = jnp.where((digit ^ k) < digit, piece, 0.0)
            before = piece_before if before is None else before + piece_before
        total = total.astype(F32) + sum(wide)
        stride *= radix


def merge_kernel(axis, stride, place, *refs):
    ins, (send_ref, keep_ref) = refs[:-2], refs[-2:]
    n, width = 2 * send_ref.shape[0], send_ref.shape[2]
    bound_refs, came_refs = ins[:n], ins[n:]
    early = None
    if len(came_refs) % 2 == 0:
        early, came_refs = came_refs[0][:, pl.ds(place, width)], came_refs[1:]
    digit = (lax.axis_index(axis) // stride) % (len(came_refs) + 1)
    for k, came_ref in enumerate(came_refs, 1):
        piece = jnp.where((digit ^ k) < digit, came_ref[:, pl.ds(place, width)].astype(F32), 0.0)
        early = piece if early is None else early + piece
    for k in range(n):
        held = early + bound_refs[k][:, pl.ds(place, width)]
        if k & 1:
            send_ref[k // 2] = held.astype(BF16)
        else:
            keep_ref[k // 2] = held


def near(value):
    return pltpu.with_memory_space_constraint(value, pltpu.VMEM)


def far(value):
    return pltpu.with_memory_space_constraint(value, pltpu.HBM)


def merged(held, got, bit):
    kept = [k for k in held if not k & bit]
    return {k: held[k] + got[i].astype(F32) for i, k in enumerate(kept)}


def cost(flops, size):
    return pl.CostEstimate(flops=flops, bytes_accessed=size, transcendentals=0)


def body(loaded, packing, pattern, w_query, w_key, w_value, norm_gain, w_out):
    n = lax.axis_size("seqi")
    rows, depth = loaded.shape
    head = depth // H
    width = min(LANES, depth)
    steps = depth // width
    cap = 2 * rows // n
    chunk = depth // CHUNKS
    square = depth * depth
    table = jnp.swapaxes(packing, 2, 3)
    smem = pl.BlockSpec(memory_space=pltpu.SMEM)
    vmem = pl.BlockSpec(memory_space=pltpu.VMEM)
    hbm = pl.BlockSpec(memory_space=pltpu.HBM)
    shape = jax.ShapeDtypeStruct
    weight = pltpu.VMEM((depth, depth), BF16)
    params = pltpu.CompilerParams(vmem_limit_bytes=VMEM)

    slots = pl.pallas_call(
        functools.partial(slot_kernel, "seqi"),
        in_specs=[smem, vmem],
        out_specs=[vmem] * (n - 1),
        out_shape=[pltpu.VMEM((cap, depth), BF16)] * (n - 1),
        compiler_params=params,
        cost_estimate=cost(SLOTS_COST, 4 * rows * depth),
        name="slots",
    )(far(table), far(loaded))
    came = []
    for k in range(1, n):
        came.append(swap(slots[k - 1], "seqi", k))
    key, value, state = pl.pallas_call(
        functools.partial(state_kernel, head, width),
        in_specs=[vmem] * 3,
        out_specs=[vmem] * 3,
        out_shape=[pltpu.VMEM((rows, depth), BF16)] * 2 + [pltpu.VMEM((head, depth), BF16)],
        compiler_params=params,
        cost_estimate=cost(4 * rows * square, 4 * square),
        name="states",
    )(loaded, w_key, w_value)
    before, groups, stride = earlier_groups(state, "seqo")
    groups = groups if before is None else [before] + groups
    bound = pl.pallas_call(
        functools.partial(bound_kernel, "seqi", head, width),
        in_specs=[smem, vmem, vmem],
        out_specs=[vmem] * n,
        out_shape=[shape((head, depth), F32)] * n,
        compiler_params=params,
        cost_estimate=cost(2 * n * rows * head * depth * 4, 4 * rows * depth),
        name="bounds",
    )(table, key, value)

    parts, gate = [], None
    for c in range(CHUNKS):
        send, keep = pl.pallas_call(
            functools.partial(merge_kernel, "seqo", stride, c * chunk),
            in_specs=[vmem] * (n + len(groups)),
            out_specs=[vmem] * 2,
            out_shape=[
                pltpu.VMEM((n // 2, head, chunk), BF16),
                pltpu.VMEM((n // 2, head, chunk), F32),
            ],
            compiler_params=params,
            cost_estimate=cost(2 * n * head * chunk, 8 * n * head * chunk),
            name="merge",
        )(*bound, *(near(piece) for piece in groups))
        got = swap(send, "seqi", 1)
        parts.append(({k: keep[k // 2] for k in range(0, n, 2)}, got))
    bit = 2
    while bit < n:
        for c, (held, got) in enumerate(parts):
            if c > 0:
                got, _ = lax.optimization_barrier((got, gate))
            held = merged(held, got, bit // 2)
            send = [held[k].astype(BF16) for k in held if k & bit]
            gate = jnp.stack(send) if len(send) > 1 else send[0][None]
            parts[c] = held, swap(gate, "seqi", bit)
        bit *= 2
    kept, last = [held[0] for held, _ in parts], [got[0] for _, got in parts]

    query, local, tokens = [], [], None
    for c in range(CHUNKS):
        if c == 0:
            specs, values = [smem] + [vmem] * (n + 4), (table, pattern, loaded, w_query, w_key, w_value, *came)
        else:
            specs, values = [vmem] * 5, (pattern, tokens, w_query, w_key, w_value)
        outs = [pltpu.VMEM((rows, chunk), BF16), pltpu.VMEM((rows, chunk), F32)]
        outs += [pltpu.VMEM((rows, depth), BF16)] if c == 0 else []
        q_part, local_part, *rest = pl.pallas_call(
            functools.partial(local_kernel, "seqi", head, width, c * chunk),
            in_specs=specs,
            out_specs=[vmem] * len(outs),
            out_shape=outs,
            compiler_params=params,
            cost_estimate=cost(6 * rows * depth * chunk, 6 * depth * chunk),
            name="local",
        )(*values)
        query.append(q_part)
        local.append(local_part)
        tokens = rest[0] if rest else tokens

    gain, total = norm_gain.reshape(1, depth), []
    for c in range(CHUNKS):
        end = c == CHUNKS - 1
        total = [
            pl.pallas_call(
                functools.partial(out_kernel, head, width, c * chunk, depth),
                in_specs=[vmem] * (6 + len(total)),
                out_specs=hbm if end else vmem,
                out_shape=shape((rows, depth), F32) if end else pltpu.VMEM((rows, depth), F32),
                scratch_shapes=[pltpu.VMEM((rows, depth), F32), pltpu.SemaphoreType.DMA((steps,))] * end,
                compiler_params=params,
                cost_estimate=cost(2 * rows * depth * chunk, 2 * depth * chunk),
                name="out",
            )(query[c], local[c], kept[c], last[c], gain, w_out, *total)
        ]
    return total[0]


def solution(mesh):
    return jax.shard_map(
        body,
        mesh=mesh,
        in_specs=(
            P(("dp", "seqo", "seqi"), None),
            P(("dp", "seqo"), None, None, None),
            P(("dp", "seqo", "seqi"), None, None),
            P(),
            P(),
            P(),
            P(),
            P(),
        ),
        out_specs=P(("dp", "seqo", "seqi"), None),
        check_vma=False,
    )
```

```python
import functools

import jax
import jax.numpy as jnp
from jax import lax
from jax.experimental import pallas as pl
from jax.experimental.pallas import tpu as pltpu
from jax.sharding import PartitionSpec as P


H = 16
EPSILON = 1e-06
LANES = 256
VMEM = 16 * 2**20
SLOTS_COST = 10**11
CHUNKS = 2


F32 = jnp.float32
BF16 = jnp.bfloat16


def mm(a, b):
    return lax.dot_general(a, b, (((1,), (0,)), ((), ())), preferred_element_type=F32)


def mm_nt(a, b):
    return lax.dot_general(a, b, (((1,), (1,)), ((), ())), preferred_element_type=F32)


def mm_tn(a, b):
    return lax.dot_general(a, b, (((0,), (0,)), ((), ())), preferred_element_type=F32)


def iota(shape, dim):
    return lax.broadcasted_iota(jnp.int32, shape, dim)


def diagonal(blocks, head):
    width = blocks.shape[1]
    heads = width // head
    rows = blocks.shape[0] // heads
    column = iota((rows, width), 1) // head
    out = jnp.zeros((rows, width), blocks.dtype)
    for i in range(heads):
        out = jnp.where(column == i, blocks[i * rows : (i + 1) * rows], out)
    return out


def state_kernel(head, width, x_ref, wk, wv, key_ref, value_ref, s_ref):
    rows = x_ref[...]
    for j in range(rows.shape[1] // width):
        cols = pl.ds(j * width, width)
        key = mm(rows, wk[:, cols]).astype(BF16)
        value = mm(rows, wv[:, cols]).astype(BF16)
        key_ref[:, cols], value_ref[:, cols] = key, value
        s_ref[:, cols] = diagonal(mm_tn(key, value), head).astype(BF16)


def slot_kernel(axis, table, x_ref, *slot_refs):
    me = lax.axis_index(axis)
    rows, cap = x_ref.shape[0], slot_refs[0].shape[0]
    slot, row = iota((cap, rows), 0), iota((cap, rows), 1)
    picks = []
    for k in range(1, len(slot_refs) + 1):
        first, count = table[0, me, 0, me ^ k], table[0, me, 1, me ^ k]
        picks.append(jnp.logical_and(row == first + slot, slot < count).astype(BF16))
    picked = mm(jnp.concatenate(picks, axis=0), x_ref[...]).astype(BF16)
    for k, slot_ref in enumerate(slot_refs):
        slot_ref[...] = picked[k * cap : (k + 1) * cap]


def bound_kernel(axis, head, width, table, key_ref, value_ref, *m_refs):
    me = lax.axis_index(axis)
    rows, depth = key_ref.shape
    row = iota((rows, width), 0)
    for j in range(depth // width):
        cols = pl.ds(j * width, width)
        key, value = key_ref[:, cols], value_ref[:, cols]
        for k, m_ref in enumerate(m_refs):
            kept = jnp.where(row < table[0, me, 0, me ^ k], value, jnp.zeros_like(value))
            m_ref[:, cols] = diagonal(mm_tn(key, kept), head)


def unpack(axis, table, x_ref, slots):
    rows, me = x_ref.shape[0], lax.axis_index(axis)
    picks, held = [], []
    for k, held_ref in enumerate((x_ref, *slots)):
        source = me ^ k
        start = jnp.int32(0)
        for s in range(len(slots) + 1):
            start += jnp.where(s < source, table[0, s, 1, me], 0)
        count = table[0, source, 1, me]
        first = table[0, me, 0, me] if k == 0 else 0
        shape = rows, held_ref.shape[0]
        row, slot = iota(shape, 0), iota(shape, 1)
        place = row - start
        pick = (slot == place + first) & (place >= 0) & (place < count)
        picks.append(pick.astype(BF16))
        held.append(held_ref[...])
    return mm(jnp.concatenate(picks, axis=1), jnp.concatenate(held, axis=0)).astype(BF16)


def local_kernel(axis, head, width, place, *refs):
    if place == 0:
        (table, pattern_ref, x_ref, wq, wk, wv, *slots), (q_ref, local_ref, tokens_ref) = refs[:-3], refs[-3:]
        x = unpack(axis, table, x_ref, slots)
        tokens_ref[...] = x
    else:
        pattern_ref, tokens_ref, wq, wk, wv, q_ref, local_ref = refs
        x = tokens_ref[...]
    rows = x.shape[0]
    frames = pattern_ref.shape[1]
    per = rows // frames
    grow = (iota((rows, frames), 0) // per == iota((rows, frames), 1)).astype(BF16)
    seen = (pattern_ref[0] > 0).astype(BF16)
    allowed = mm_nt(mm(grow, seen).astype(BF16), grow) > 0.5
    heads = width // head
    column = iota((rows, width), 1) // head
    for j in range(q_ref.shape[1] // width):
        inner, cols = pl.ds(j * width, width), pl.ds(place + j * width, width)
        query = mm(x, wq[:, cols]).astype(BF16)
        key = mm(x, wk[:, cols]).astype(BF16)
        value = mm(x, wv[:, cols]).astype(BF16)
        zero = jnp.zeros_like(query)
        stacked = jnp.concatenate([jnp.where(column == i, query, zero) for i in range(heads)], axis=0)
        scores = mm_nt(stacked, key)
        masked = jnp.concatenate(
            [jnp.where(allowed, scores[i * rows : (i + 1) * rows], 0.0) for i in range(heads)], axis=0
        ).astype(BF16)
        local_ref[:, inner] = diagonal(mm(masked, value), head)
        q_ref[:, inner] = query


def out_kernel(head, width, place, depth, steps, q_ref, local_ref, gain_ref, w, final_ref, kept_ref, *rest):
    chunk = final_ref.shape[1]
    landed, rest = rest[:steps], rest[steps:]
    so_far, rest = (rest[0], rest[1:]) if place > 0 else (None, rest)
    heads = width // head
    same = iota((width, width), 0) // head == iota((width, width), 1) // head
    ones = same.astype(BF16)
    zero = jnp.zeros((width, width), BF16)
    normed = []
    for j in range(chunk // width):
        inner, cols = pl.ds(j * width, width), pl.ds(place + j * width, width)
        prefix = kept_ref[:, cols] + final_ref[:, inner].astype(F32)
        for ref in landed:
            prefix = prefix + ref[:, cols].astype(F32)
        high = prefix.astype(BF16)
        low = (prefix - high.astype(F32)).astype(BF16)
        query = q_ref[:, inner]
        attended = local_ref[:, inner]
        for part in (high, low):
            spread = jnp.where(same, jnp.concatenate([part] * heads, axis=0), zero)
            attended = attended + mm(query, spread)
        square = attended * attended
        sq_high = square.astype(BF16)
        sq_low = (square - sq_high.astype(F32)).astype(BF16)
        mean = (mm(sq_high, ones) + mm(sq_low, ones)) * (1.0 / head)
        normed.append((attended * lax.rsqrt(mean + EPSILON) * gain_ref[:, cols]).astype(BF16))
    normed = jnp.concatenate(normed, axis=1)
    copies = []
    for j in range(depth // width):
        cols = pl.ds(j * width, width)
        piece = mm(normed, w[pl.ds(place, chunk), cols])
        piece = piece if so_far is None else so_far[:, cols] + piece
        if place + chunk < depth:
            rest[0][:, cols] = piece
        else:
            out_hbm, total, sems = rest
            total[:, cols] = piece
            copies.append(pltpu.make_async_copy(total.at[:, cols], out_hbm.at[:, cols], sems.at[j]))
            copies[j].start()
    for copy in copies:
        copy.wait()


def swap(value, axis, bits):
    return lax.ppermute(value, axis, [(i, i ^ bits) for i in range(lax.axis_size(axis))])


def earlier_groups(state, axis):
    count, mine = lax.axis_size(axis), lax.axis_index(axis)
    before, total, stride = None, state, 1
    while True:
        radix = min(4, count // stride)
        came = []
        for k in range(1, radix):
            came.append(swap(total.astype(BF16), axis, k * stride))
        if stride * radix >= count:
            return before, came, stride
        digit = (mine // stride) % radix
        wide = [piece.astype(F32) for piece in came]
        for k, piece in enumerate(wide, 1):
            piece_before = jnp.where((digit ^ k) < digit, piece, 0.0)
            before = piece_before if before is None else before + piece_before
        total = total.astype(F32) + sum(wide)
        stride *= radix


def merge_kernel(axis, stride, n, *refs):
    bound_refs, came_refs, outs = refs[:n], list(refs[n : -(n // 2 + 2)]), refs[-(n // 2 + 2) :]
    early = None
    if len(came_refs) % 2 == 0:
        early = came_refs.pop(0)[...]
    digit = (lax.axis_index(axis) // stride) % (len(came_refs) + 1)
    for k, came_ref in enumerate(came_refs, 1):
        piece = jnp.where((digit ^ k) < digit, came_ref[...].astype(F32), 0.0)
        early = piece if early is None else early + piece
    for k in range(n):
        held = early + bound_refs[k][...]
        if k % 2 == 0:
            outs[2 + k // 2][...] = held
        elif k == 1:
            outs[1][...] = held.astype(BF16)
        else:
            outs[0][k // 2 - 1] = held.astype(BF16)


def near(value):
    return pltpu.with_memory_space_constraint(value, pltpu.VMEM)


def far(value):
    return pltpu.with_memory_space_constraint(value, pltpu.HBM)


def cost(flops, size):
    return pl.CostEstimate(flops=flops, bytes_accessed=size, transcendentals=0)


def body(loaded, packing, pattern, w_query, w_key, w_value, norm_gain, w_out):
    n = lax.axis_size("seqi")
    rows, depth = loaded.shape
    head = depth // H
    width = min(LANES, depth)
    steps = depth // width
    cap = 2 * rows // n
    chunk = depth // CHUNKS
    square = depth * depth
    table = jnp.swapaxes(packing, 2, 3)
    smem = pl.BlockSpec(memory_space=pltpu.SMEM)
    vmem = pl.BlockSpec(memory_space=pltpu.VMEM)
    hbm = pl.BlockSpec(memory_space=pltpu.HBM)
    shape = jax.ShapeDtypeStruct
    weight = pltpu.VMEM((depth, depth), BF16)
    params = pltpu.CompilerParams(vmem_limit_bytes=VMEM)

    slots = pl.pallas_call(
        functools.partial(slot_kernel, "seqi"),
        in_specs=[smem, vmem],
        out_specs=[vmem] * (n - 1),
        out_shape=[pltpu.VMEM((cap, depth), BF16)] * (n - 1),
        compiler_params=params,
        cost_estimate=cost(SLOTS_COST, 4 * rows * depth),
        name="slots",
    )(far(table), far(loaded))
    came = []
    for k in range(1, n):
        came.append(swap(slots[k - 1], "seqi", k))
    key, value, state = pl.pallas_call(
        functools.partial(state_kernel, head, width),
        in_specs=[vmem] * 3,
        out_specs=[vmem] * 3,
        out_shape=[pltpu.VMEM((rows, depth), BF16)] * 2 + [pltpu.VMEM((head, depth), BF16)],
        compiler_params=params,
        cost_estimate=cost(4 * rows * square, 4 * square),
        name="states",
    )(loaded, w_key, w_value)
    before, groups, stride = earlier_groups(state, "seqo")
    groups = groups if before is None else [before] + groups
    bound = pl.pallas_call(
        functools.partial(bound_kernel, "seqi", head, width),
        in_specs=[smem, vmem, vmem],
        out_specs=[vmem] * n,
        out_shape=[shape((head, depth), F32)] * n,
        compiler_params=params,
        cost_estimate=cost(2 * n * rows * head * depth * 4, 4 * rows * depth),
        name="bounds",
    )(table, key, value)

    onward, last, *keep = pl.pallas_call(
        functools.partial(merge_kernel, "seqo", stride, n),
        in_specs=[vmem] * (n + len(groups)),
        out_specs=[vmem] * (n // 2 + 2),
        out_shape=[pltpu.VMEM((n // 2 - 1, head, depth), BF16), pltpu.VMEM((head, depth), BF16)]
        + [pltpu.VMEM((head, depth), F32)] * (n // 2),
        compiler_params=params,
        cost_estimate=cost(2 * n * head * depth, 8 * n * head * depth),
        name="merge",
    )(*bound, *(near(piece) for piece in groups))
    held, last, bit = {2 * i: value for i, value in enumerate(keep)}, [last], 1
    kept, held, landed = held[0], {k: value for k, value in held.items() if k}, []
    while held:
        handed = swap(onward, "seqi", bit)
        landed.append(swap(last[0], "seqi", bit))
        held = {k: value + handed[i].astype(F32) for i, (k, value) in enumerate(held.items())}
        bit *= 2
        last = [held.pop(bit).astype(BF16)]
        more = [held.pop(k).astype(BF16) for k in list(held) if k & bit]
        onward = jnp.stack(more) if more else None
    final = []
    for c in range(CHUNKS):
        final.append(swap(last[0][:, c * chunk : (c + 1) * chunk], "seqi", bit))

    query, local, tokens = [], [], None
    for c in range(CHUNKS):
        if c == 0:
            specs, values = [smem] + [vmem] * (n + 4), (table, pattern, loaded, w_query, w_key, w_value, *came)
        else:
            specs, values = [vmem] * 5, (pattern, tokens, w_query, w_key, w_value)
        outs = [pltpu.VMEM((rows, chunk), BF16), pltpu.VMEM((rows, chunk), F32)]
        outs += [pltpu.VMEM((rows, depth), BF16)] if c == 0 else []
        q_part, local_part, *rest = pl.pallas_call(
            functools.partial(local_kernel, "seqi", head, width, c * chunk),
            in_specs=specs,
            out_specs=[vmem] * len(outs),
            out_shape=outs,
            compiler_params=params,
            cost_estimate=cost(6 * rows * depth * chunk, 6 * depth * chunk),
            name="local",
        )(*values)
        query.append(q_part)
        local.append(local_part)
        tokens = rest[0] if rest else tokens

    gain, total = norm_gain.reshape(1, depth), []
    for c in range(CHUNKS):
        end = c == CHUNKS - 1
        total = [
            pl.pallas_call(
                functools.partial(out_kernel, head, width, c * chunk, depth, len(landed)),
                in_specs=[vmem] * (6 + len(landed) + len(total)),
                out_specs=hbm if end else vmem,
                out_shape=shape((rows, depth), F32) if end else pltpu.VMEM((rows, depth), F32),
                scratch_shapes=[pltpu.VMEM((rows, depth), F32), pltpu.SemaphoreType.DMA((steps,))] * end,
                compiler_params=params,
                cost_estimate=cost(2 * rows * depth * chunk, 2 * depth * chunk),
                name="out",
            )(query[c], local[c], gain, w_out, final[c], kept, *landed, *total)
        ]
    return total[0]


def solution(mesh):
    return jax.shard_map(
        body,
        mesh=mesh,
        in_specs=(
            P(("dp", "seqo", "seqi"), None),
            P(("dp", "seqo"), None, None, None),
            P(("dp", "seqo", "seqi"), None, None),
            P(),
            P(),
            P(),
            P(),
            P(),
        ),
        out_specs=P(("dp", "seqo", "seqi"), None),
        check_vma=False,
    )
```

```python
import functools

import jax
import jax.numpy as jnp
from jax import lax
from jax.experimental import pallas as pl
from jax.experimental.pallas import tpu as pltpu
from jax.sharding import PartitionSpec as P


H = 16
EPSILON = 1e-06
LANES = 256
VMEM = 16 * 2**20
SLOTS_COST = 10**11
CHUNKS = 2


F32 = jnp.float32
BF16 = jnp.bfloat16


def mm(a, b):
    return lax.dot_general(a, b, (((1,), (0,)), ((), ())), preferred_element_type=F32)


def mm_nt(a, b):
    return lax.dot_general(a, b, (((1,), (1,)), ((), ())), preferred_element_type=F32)


def mm_tn(a, b):
    return lax.dot_general(a, b, (((0,), (0,)), ((), ())), preferred_element_type=F32)


def iota(shape, dim):
    return lax.broadcasted_iota(jnp.int32, shape, dim)


def diagonal(blocks, head):
    width = blocks.shape[1]
    heads = width // head
    rows = blocks.shape[0] // heads
    column = iota((rows, width), 1) // head
    out = jnp.zeros((rows, width), blocks.dtype)
    for i in range(heads):
        out = jnp.where(column == i, blocks[i * rows : (i + 1) * rows], out)
    return out


def state_kernel(head, width, x_ref, wk, wv, key_ref, value_ref, s_ref):
    rows = x_ref[...]
    for j in range(rows.shape[1] // width):
        cols = pl.ds(j * width, width)
        key = mm(rows, wk[:, cols]).astype(BF16)
        value = mm(rows, wv[:, cols]).astype(BF16)
        key_ref[:, cols], value_ref[:, cols] = key, value
        s_ref[:, cols] = diagonal(mm_tn(key, value), head).astype(BF16)


def slot_kernel(axis, table, x_ref, *slot_refs):
    me = lax.axis_index(axis)
    rows, cap = x_ref.shape[0], slot_refs[0].shape[0]
    slot, row = iota((cap, rows), 0), iota((cap, rows), 1)
    picks = []
    for k in range(1, len(slot_refs) + 1):
        first, count = table[0, me, 0, me ^ k], table[0, me, 1, me ^ k]
        picks.append(jnp.logical_and(row == first + slot, slot < count).astype(BF16))
    picked = mm(jnp.concatenate(picks, axis=0), x_ref[...]).astype(BF16)
    for k, slot_ref in enumerate(slot_refs):
        slot_ref[...] = picked[k * cap : (k + 1) * cap]


def bound_kernel(axis, head, width, table, key_ref, value_ref, *m_refs):
    me = lax.axis_index(axis)
    rows, depth = key_ref.shape
    row = iota((rows, width), 0)
    for j in range(depth // width):
        cols = pl.ds(j * width, width)
        key, value = key_ref[:, cols], value_ref[:, cols]
        for k, m_ref in enumerate(m_refs):
            kept = jnp.where(row < table[0, me, 0, me ^ k], value, jnp.zeros_like(value))
            m_ref[:, cols] = diagonal(mm_tn(key, kept), head)


def unpack(axis, table, x_ref, slots):
    rows, me = x_ref.shape[0], lax.axis_index(axis)
    picks, held = [], []
    for k, held_ref in enumerate((x_ref, *slots)):
        source = me ^ k
        start = jnp.int32(0)
        for s in range(len(slots) + 1):
            start += jnp.where(s < source, table[0, s, 1, me], 0)
        count = table[0, source, 1, me]
        first = table[0, me, 0, me] if k == 0 else 0
        shape = rows, held_ref.shape[0]
        row, slot = iota(shape, 0), iota(shape, 1)
        place = row - start
        pick = (slot == place + first) & (place >= 0) & (place < count)
        picks.append(pick.astype(BF16))
        held.append(held_ref[...])
    return mm(jnp.concatenate(picks, axis=1), jnp.concatenate(held, axis=0)).astype(BF16)


def local_kernel(axis, head, width, place, *refs):
    if place == 0:
        (table, pattern_ref, x_ref, wq, wk, wv, *slots), (q_ref, local_ref, tokens_ref) = refs[:-3], refs[-3:]
        x = unpack(axis, table, x_ref, slots)
        tokens_ref[...] = x
    else:
        pattern_ref, tokens_ref, wq, wk, wv, q_ref, local_ref = refs
        x = tokens_ref[...]
    rows = x.shape[0]
    frames = pattern_ref.shape[1]
    per = rows // frames
    grow = (iota((rows, frames), 0) // per == iota((rows, frames), 1)).astype(BF16)
    seen = (pattern_ref[0] > 0).astype(BF16)
    allowed = mm_nt(mm(grow, seen).astype(BF16), grow) > 0.5
    heads = width // head
    column = iota((rows, width), 1) // head
    for j in range(q_ref.shape[1] // width):
        inner, cols = pl.ds(j * width, width), pl.ds(place + j * width, width)
        query = mm(x, wq[:, cols]).astype(BF16)
        key = mm(x, wk[:, cols]).astype(BF16)
        value = mm(x, wv[:, cols]).astype(BF16)
        zero = jnp.zeros_like(query)
        stacked = jnp.concatenate([jnp.where(column == i, query, zero) for i in range(heads)], axis=0)
        scores = mm_nt(stacked, key)
        masked = jnp.concatenate(
            [jnp.where(allowed, scores[i * rows : (i + 1) * rows], 0.0) for i in range(heads)], axis=0
        ).astype(BF16)
        local_ref[:, inner] = diagonal(mm(masked, value), head)
        q_ref[:, inner] = query


def spread(part, heads, same):
    return jnp.where(same, jnp.concatenate([part] * heads, axis=0), jnp.zeros(same.shape, BF16))


def carry_kernel(head, width, chunks, kept_ref, *refs):
    queries, locals_, landed, outs = refs[:chunks], refs[chunks : 2 * chunks], refs[2 * chunks : -chunks], refs[-chunks:]
    same = iota((width, width), 0) // head == iota((width, width), 1) // head
    chunk = outs[0].shape[1]
    for j in range(kept_ref.shape[1] // width):
        c, place = divmod(j * width, chunk)
        cols, inner = pl.ds(j * width, width), pl.ds(place, width)
        prefix = kept_ref[:, cols]
        for ref in landed:
            prefix = prefix + ref[:, cols].astype(F32)
        high = prefix.astype(BF16)
        low = (prefix - high.astype(F32)).astype(BF16)
        attended = locals_[c][:, inner]
        for part in (high, low):
            attended = attended + mm(queries[c][:, inner], spread(part, width // head, same))
        outs[c][:, inner] = attended


def out_kernel(head, width, place, depth, q_ref, local_ref, gain_ref, w, final_ref, *rest):
    chunk = final_ref.shape[1]
    so_far, rest = (rest[0], rest[1:]) if place > 0 else (None, rest)
    heads = width // head
    same = iota((width, width), 0) // head == iota((width, width), 1) // head
    ones = same.astype(BF16)
    normed = []
    for j in range(chunk // width):
        inner, cols = pl.ds(j * width, width), pl.ds(place + j * width, width)
        attended = local_ref[:, inner] + mm(q_ref[:, inner], spread(final_ref[:, inner], heads, same))
        square = attended * attended
        sq_high = square.astype(BF16)
        sq_low = (square - sq_high.astype(F32)).astype(BF16)
        mean = (mm(sq_high, ones) + mm(sq_low, ones)) * (1.0 / head)
        normed.append((attended * lax.rsqrt(mean + EPSILON) * gain_ref[:, cols]).astype(BF16))
    normed = jnp.concatenate(normed, axis=1)
    copies = []
    for j in range(depth // width):
        cols = pl.ds(j * width, width)
        piece = mm(normed, w[pl.ds(place, chunk), cols])
        piece = piece if so_far is None else so_far[:, cols] + piece
        if place + chunk < depth:
            rest[0][:, cols] = piece
        else:
            out_hbm, total, sems = rest
            total[:, cols] = piece
            copies.append(pltpu.make_async_copy(total.at[:, cols], out_hbm.at[:, cols], sems.at[j]))
            copies[j].start()
    for copy in copies:
        copy.wait()


def swap(value, axis, bits):
    return lax.ppermute(value, axis, [(i, i ^ bits) for i in range(lax.axis_size(axis))])


def earlier_groups(state, axis):
    count, mine = lax.axis_size(axis), lax.axis_index(axis)
    before, total, stride = None, state, 1
    while True:
        radix = min(4, count // stride)
        came = []
        for k in range(1, radix):
            came.append(swap(total.astype(BF16), axis, k * stride))
        if stride * radix >= count:
            return before, came, stride
        digit = (mine // stride) % radix
        wide = [piece.astype(F32) for piece in came]
        for k, piece in enumerate(wide, 1):
            piece_before = jnp.where((digit ^ k) < digit, piece, 0.0)
            before = piece_before if before is None else before + piece_before
        total = total.astype(F32) + sum(wide)
        stride *= radix


def merge_kernel(axis, stride, n, *refs):
    bound_refs, came_refs, outs = refs[:n], list(refs[n : -(n // 2 + 2)]), refs[-(n // 2 + 2) :]
    early = None
    if len(came_refs) % 2 == 0:
        early = came_refs.pop(0)[...]
    digit = (lax.axis_index(axis) // stride) % (len(came_refs) + 1)
    for k, came_ref in enumerate(came_refs, 1):
        piece = jnp.where((digit ^ k) < digit, came_ref[...].astype(F32), 0.0)
        early = piece if early is None else early + piece
    for k in range(n):
        held = early + bound_refs[k][...]
        if k % 2 == 0:
            outs[2 + k // 2][...] = held
        elif k == 1:
            outs[1][...] = held.astype(BF16)
        else:
            outs[0][k // 2 - 1] = held.astype(BF16)


def near(value):
    return pltpu.with_memory_space_constraint(value, pltpu.VMEM)


def far(value):
    return pltpu.with_memory_space_constraint(value, pltpu.HBM)


def cost(flops, size):
    return pl.CostEstimate(flops=flops, bytes_accessed=size, transcendentals=0)


def body(loaded, packing, pattern, w_query, w_key, w_value, norm_gain, w_out):
    n = lax.axis_size("seqi")
    rows, depth = loaded.shape
    head = depth // H
    width = min(LANES, depth)
    steps = depth // width
    cap = 2 * rows // n
    chunk = depth // CHUNKS
    square = depth * depth
    table = jnp.swapaxes(packing, 2, 3)
    smem = pl.BlockSpec(memory_space=pltpu.SMEM)
    vmem = pl.BlockSpec(memory_space=pltpu.VMEM)
    hbm = pl.BlockSpec(memory_space=pltpu.HBM)
    shape = jax.ShapeDtypeStruct
    weight = pltpu.VMEM((depth, depth), BF16)
    params = pltpu.CompilerParams(vmem_limit_bytes=VMEM)

    slots = pl.pallas_call(
        functools.partial(slot_kernel, "seqi"),
        in_specs=[smem, vmem],
        out_specs=[vmem] * (n - 1),
        out_shape=[pltpu.VMEM((cap, depth), BF16)] * (n - 1),
        compiler_params=params,
        cost_estimate=cost(SLOTS_COST, 4 * rows * depth),
        name="slots",
    )(far(table), far(loaded))
    came = []
    for k in range(1, n):
        came.append(swap(slots[k - 1], "seqi", k))
    key, value, state = pl.pallas_call(
        functools.partial(state_kernel, head, width),
        in_specs=[vmem] * 3,
        out_specs=[vmem] * 3,
        out_shape=[pltpu.VMEM((rows, depth), BF16)] * 2 + [pltpu.VMEM((head, depth), BF16)],
        compiler_params=params,
        cost_estimate=cost(4 * rows * square, 4 * square),
        name="states",
    )(loaded, w_key, w_value)
    before, groups, stride = earlier_groups(state, "seqo")
    groups = groups if before is None else [before] + groups
    bound = pl.pallas_call(
        functools.partial(bound_kernel, "seqi", head, width),
        in_specs=[smem, vmem, vmem],
        out_specs=[vmem] * n,
        out_shape=[shape((head, depth), F32)] * n,
        compiler_params=params,
        cost_estimate=cost(2 * n * rows * head * depth * 4, 4 * rows * depth),
        name="bounds",
    )(table, key, value)

    onward, last, *keep = pl.pallas_call(
        functools.partial(merge_kernel, "seqo", stride, n),
        in_specs=[vmem] * (n + len(groups)),
        out_specs=[vmem] * (n // 2 + 2),
        out_shape=[pltpu.VMEM((n // 2 - 1, head, depth), BF16), pltpu.VMEM((head, depth), BF16)]
        + [pltpu.VMEM((head, depth), F32)] * (n // 2),
        compiler_params=params,
        cost_estimate=cost(2 * n * head * depth, 8 * n * head * depth),
        name="merge",
    )(*bound, *(near(piece) for piece in groups))
    held, last, bit = {2 * i: value for i, value in enumerate(keep)}, [last], 1
    kept, held, landed = held[0], {k: value for k, value in held.items() if k}, []
    while held:
        handed = swap(onward, "seqi", bit)
        landed.append(swap(last[0], "seqi", bit))
        held = {k: value + handed[i].astype(F32) for i, (k, value) in enumerate(held.items())}
        bit *= 2
        last = [held.pop(bit).astype(BF16)]
        more = [held.pop(k).astype(BF16) for k in list(held) if k & bit]
        onward = jnp.stack(more) if more else None
    final = []
    for c in range(CHUNKS):
        final.append(swap(last[0][:, c * chunk : (c + 1) * chunk], "seqi", bit))

    query, local, tokens = [], [], None
    for c in range(CHUNKS):
        if c == 0:
            specs, values = [smem] + [vmem] * (n + 4), (table, pattern, loaded, w_query, w_key, w_value, *came)
        else:
            specs, values = [vmem] * 5, (pattern, tokens, w_query, w_key, w_value)
        outs = [pltpu.VMEM((rows, chunk), BF16), pltpu.VMEM((rows, chunk), F32)]
        outs += [pltpu.VMEM((rows, depth), BF16)] if c == 0 else []
        q_part, local_part, *rest = pl.pallas_call(
            functools.partial(local_kernel, "seqi", head, width, c * chunk),
            in_specs=specs,
            out_specs=[vmem] * len(outs),
            out_shape=outs,
            compiler_params=params,
            cost_estimate=cost(6 * rows * depth * chunk, 6 * depth * chunk),
            name="local",
        )(*values)
        query.append(q_part)
        local.append(local_part)
        tokens = rest[0] if rest else tokens

    local = pl.pallas_call(
        functools.partial(carry_kernel, head, width, CHUNKS),
        in_specs=[vmem] * (1 + 2 * CHUNKS + len(landed)),
        out_specs=[vmem] * CHUNKS,
        out_shape=[pltpu.VMEM((rows, chunk), F32)] * CHUNKS,
        compiler_params=params,
        cost_estimate=cost(4 * rows * depth * width, 8 * rows * depth),
        name="carry",
    )(kept, *query, *local, *landed)
    gain, total = norm_gain.reshape(1, depth), []
    for c in range(CHUNKS):
        end = c == CHUNKS - 1
        total = [
            pl.pallas_call(
                functools.partial(out_kernel, head, width, c * chunk, depth),
                in_specs=[vmem] * (5 + len(total)),
                out_specs=hbm if end else vmem,
                out_shape=shape((rows, depth), F32) if end else pltpu.VMEM((rows, depth), F32),
                scratch_shapes=[pltpu.VMEM((rows, depth), F32), pltpu.SemaphoreType.DMA((steps,))] * end,
                compiler_params=params,
                cost_estimate=cost(2 * rows * depth * chunk, 2 * depth * chunk),
                name="out",
            )(query[c], local[c], gain, w_out, final[c], *total)
        ]
    return total[0]


def solution(mesh):
    return jax.shard_map(
        body,
        mesh=mesh,
        in_specs=(
            P(("dp", "seqo", "seqi"), None),
            P(("dp", "seqo"), None, None, None),
            P(("dp", "seqo", "seqi"), None, None),
            P(),
            P(),
            P(),
            P(),
            P(),
        ),
        out_specs=P(("dp", "seqo", "seqi"), None),
        check_vma=False,
    )
```
